32 devices in a mesh: row: 4 (over y, x), col: 8 (over z, core).
Axes of the slice: x: 2, y: 2, z: 4, core: 2. Of those that a mesh axis runs over, the one named last changes fastest.
Arguments:
- mode_profiles: bfloat16 [32768, 2048], P(('row', 'col')), may hold values from -0.032958984 to 0.032958984
- region_labels: int32 [32768], P(('row', 'col')), may hold values from 0 to 15
- gain_table: float32 [16], replicated, may hold values from 0.25 to 2
- index_table: float32 [16], replicated, may hold values from -2 to 2
- field_in: bfloat16 [2048, 2048], P('row', 'col'), may hold values from -2 to 2
Outputs:
- field_out: bfloat16 [2048, 2048], P('row', 'col')
The draws below stay inside these ranges and needn't reach their ends.
All inputs are finite; a program needn't handle non-finite values.
Results may differ from the reference program's by a relative error of at most 0.02.
Values may be sent and summed in bfloat16 or wider, within the bound.
A program may use at most 64 MiB of HBM per device.

```python
import math
import jax
import jax.numpy as jnp
from jax import lax

MODES = 2048
REGIONS = 16
TERMS = 6
POINTS = 32768


def touch_ends(result, key, least, largest):
    index_at = [jax.random.randint(jax.random.fold_in(key, axis), (), 0, length) for axis, length in enumerate(result.shape)]
    main_axis = result.shape.index(max(result.shape))
    beside = index_at[:main_axis] + [(index_at[main_axis] + 1) % result.shape[main_axis]] + index_at[main_axis + 1:]
    return result.at[tuple(index_at)].set(least).at[tuple(beside)].set(largest)


def strengthened(result, rng, source, target, shards_of, factor):
    def block_of(axis_at):
        return (jnp.arange(result.shape[axis_at]) // (result.shape[axis_at] // shards_of)).reshape((-1,) + (1,) * (result.ndim - 1 - axis_at))

    near = jax.random.permutation(rng, shards_of)[block_of(target)]
    other_side = (block_of(target) + shards_of // 2) % shards_of
    return jnp.where((block_of(source) == near) | (block_of(source) == other_side), factor * result, result)


def level_of(own_key, shape, cuts, least, largest):
    def one(axis_at, parts):
        heights = jax.random.uniform(jax.random.fold_in(jax.random.fold_in(own_key, 6), axis_at), (parts,), jnp.float32, least / len(cuts), largest / len(cuts))
        return jnp.repeat(jnp.exp(heights), shape[axis_at] // parts).reshape((-1,) + (1,) * (len(shape) - axis_at - 1))

    gain = one(*cuts[0])
    for cut in cuts[1:]:
        gain = gain * one(*cut)
    return gain


def bell_draw(key, dims, width, limit, shards=(), held_as=jnp.bfloat16):
    loudness = level_of(key, dims, shards, -0.22, 0.18) if shards else 1.0
    values = jax.random.normal(key, dims, jnp.float32) * width * loudness
    return jnp.minimum(jnp.maximum(values, -limit), limit).astype(held_as)


def gaussian_with(stream_key, extent, scale, reach, shards, heavy, held_as=jnp.bfloat16):
    values = scale * jax.random.normal(stream_key, extent, jnp.float32)
    if shards:
        values = values * level_of(stream_key, extent, shards, -0.22, 0.18)
    return jnp.clip(strengthened(values, jax.random.fold_in(stream_key, 3), *heavy), -reach, reach).astype(held_as)


def setup_inputs(seed: int = 0) -> dict:
    keys = jax.random.split(jax.random.key(seed), 6)
    return {
        "mode_profiles": gaussian_with(keys[0], (POINTS, MODES), (POINTS ** -0.5), 0.032958984, ((0, 32),), (0, 1, 32, 2.75)),
        "region_labels": touch_ends(jax.random.randint(keys[1], (POINTS,), 0, REGIONS), jax.random.fold_in(keys[1], 1), 0, REGIONS - 1).astype(jnp.int32),
        "gain_table": jnp.clip(jnp.exp(jax.random.uniform(keys[2], (REGIONS,), jnp.float32, math.log(0.25), math.log(2.0))), 0.25, 2.0),
        "index_table": jnp.clip(jax.random.uniform(keys[3], (REGIONS,), jnp.float32, -2.0, 2.0), -2.0, 2.0),
        "field_in": bell_draw(keys[4], (MODES, MODES), 0.3, 2.0, ((0, 4), (1, 8))),
    }


def reference(mode_profiles, region_labels, gain_table, index_table, field_in):
    table = gain_table + index_table
    weight = table[region_labels]
    profiles = mode_profiles.astype(jnp.float32)
    scaled = (profiles * weight[:, None]).astype(jnp.bfloat16)
    coupling = jnp.dot(profiles.T, scaled.astype(jnp.float32), precision=lax.Precision.HIGHEST, preferred_element_type=jnp.float32)
    coupling = coupling.astype(jnp.bfloat16)
    start = field_in.astype(jnp.float32)
    carry = field_in
    for order in range(TERMS, 0, -1):
        product = jnp.dot(coupling, carry, preferred_element_type=jnp.float32)
        carry = (start + (1.0 / order) * product).astype(jnp.bfloat16)
    return carry
```

```python
import functools

import jax
import jax.numpy as jnp
from jax import lax
from jax.experimental import pallas as pl
from jax.experimental.pallas import tpu as pltpu
from jax.sharding import PartitionSpec as P

TERMS = 6
LANES = 128
MESH = pl.DeviceIdType.MESH


def lowest_bit(g):
    t = 0
    while not (g >> t) & 1:
        t += 1
    return t


def kernel(R, Z, n, p_ref, w_ref, f_ref, out_ref, s2, part, r0, rt, rz, cx, x0, xs, ot, send_sem, recv_sem):
    bits = R.bit_length() - 1
    blocks = n // LANES
    half = blocks // 2
    width = (half + 1) * LANES
    depth = n // (R * Z * 2)
    mine_cols = x0.shape[0]
    row_rows = n // R
    row, col = lax.axis_index("row"), lax.axis_index("col")
    z, h = col // 2, col % 2
    partner = (row, z * 2 + 1 - h)

    def flip(r, t):
        mask0, mask1 = 1 << t, 1 << (bits - 1 - t)
        mask = mask0 + h * (mask1 - mask0)
        return r + mask * (1 - 2 * ((r // mask) % 2))

    def row_of(g):
        r = row
        for t in range(bits):
            if (g >> t) & 1:
                r = flip(r, t)
        return r

    def mirrored(g):
        return sum(((g >> t) & 1) << (bits - 1 - t) for t in range(bits))

    def z_of(j):
        return (z + 1 + j) % Z

    def strip_of(r, zz, hh):
        return (r * Z + zz) * 2 + hh

    def rows_of(ref, s):
        return ref.at[pl.ds(pl.multiple_of(s * depth, depth), depth), :]

    def window_of(s):
        start = pl.multiple_of((s * depth // LANES) * LANES, LANES)
        return cx.at[pl.ds(pl.multiple_of(s * depth, depth), depth), pl.ds(start, width)]

    ids, started = {}, []

    def slot(key):
        return ids.setdefault(key, len(ids))

    def send(src, dst, device, key):
        copy = pltpu.make_async_remote_copy(
            src_ref=src, dst_ref=dst, send_sem=send_sem.at[len(started)],
            recv_sem=recv_sem.at[slot(key)], device_id=device, device_id_type=MESH)
        copy.start()
        started.append(copy)

    def arrived(ref, key):
        pltpu.make_async_remote_copy(
            src_ref=ref, dst_ref=ref, send_sem=send_sem.at[0],
            recv_sem=recv_sem.at[slot(key)], device_id=partner, device_id_type=MESH).wait_recv()

    barrier = pltpu.get_barrier_semaphore()
    peers = [((row + k) % R, col) for k in range(1, R)]
    peers += [(row, ((z + k) % Z) * 2 + h) for k in range(1, Z)] + [partner]
    for peer in peers:
        pl.semaphore_signal(barrier, inc=1, device_id=peer, device_id_type=MESH)
    pl.semaphore_wait(barrier, len(peers))

    def columns_at(r):
        return pl.ds(pl.multiple_of(r * row_rows, row_rows), row_rows)

    def slab_at(r):
        return pl.ds(pl.multiple_of(r * mine_cols, mine_cols), mine_cols)

    for k in range(1, R):
        to = (row + k) % R
        send(f_ref.at[slab_at(to), :], x0.at[:, columns_at(row)], (to, col), ("field", k))
    x0[:, columns_at(row)] = f_ref[slab_at(row), :]

    scaled = (p_ref[...].astype(jnp.float32) * w_ref[...]).astype(jnp.bfloat16)
    s2[:, :n] = scaled
    s2[:, n:] = scaled[:, : width - LANES]

    order = sorted(range(R), key=lambda g: (lowest_bit(g) if g else bits, -g))
    pair = 2 * LANES
    for g in order:
        r = row_of(g)

        @pl.loop(0, row_rows // pair)
        def _(q):
            base = pl.multiple_of(r * row_rows + q * pair, pair)
            left = p_ref[:, pl.ds(base, pair)].T
            both = jnp.dot(left, s2[:, pl.ds(base, width + LANES)], preferred_element_type=jnp.float32)
            part[pl.ds(base, LANES), :] = both[:LANES, :width].astype(jnp.bfloat16)
            part[pl.ds(base + LANES, LANES), :] = both[LANES:, LANES:].astype(jnp.bfloat16)

        for j in range(Z):
            send(rows_of(part, strip_of(r, z_of(j), 1 - h)), r0.at[mirrored(g) * Z + j], partner, ("core", mirrored(g), j))
            ids.setdefault(("core", g, j), len(ids))

    stage_slot = {}
    for t in range(bits):
        for g in range(R):
            if g % (2 << t) == 0:
                stage_slot[t, g] = len(stage_slot)

    for g in order:
        r = row_of(g)
        low = lowest_bit(g) if g else bits
        for j in range(Z):
            arrived(r0.at[g * Z + j], ("core", g, j))
            own = rows_of(part, strip_of(r, z_of(j), h))
            total = own[...].astype(jnp.float32) + r0[g * Z + j].astype(jnp.float32)
            for t in range(low):
                piece = rt.at[stage_slot[t, g] * Z + j]
                arrived(piece, ("row", t, g, j))
                total = total + piece[...].astype(jnp.float32)
            if g:
                own[...] = total.astype(jnp.bfloat16)
                seen = g ^ (1 << low)
                send(own, rt.at[stage_slot[low, seen] * Z + j], (flip(row, low), col), ("row", low, seen, j))
            elif j < Z - 1:
                own[...] = total.astype(jnp.bfloat16)
                send(own, rz.at[j], (row, z_of(j) * 2 + h), ("z", j))
            else:
                for i in range(Z - 1):
                    arrived(rz.at[i], ("z", i))
                    total = total + rz[i].astype(jnp.float32)
                window_of(strip_of(row, z, h))[...] = total.astype(jnp.bfloat16)

    def spread(g, strip, key_j):
        low = lowest_bit(g) if g else bits
        view = window_of(strip)
        for t in reversed(range(low)):
            send(view, view, (flip(row, t), col), ("spread", g | (1 << t), key_j))
        send(view, view, partner, ("spread_core", mirrored(g), key_j))

    mine = window_of(strip_of(row, z, h))
    for j in range(Z - 1):
        send(mine, mine, (row, z_of(j) * 2 + h), ("spread", 0, j + 1))
    for j in range(Z):
        for g in range(R):
            low = lowest_bit(g) if g else bits
            source_z = (z + Z - j) % Z
            strip = strip_of(row_of(g), source_z, h)
            if g or j:
                arrived(window_of(strip), ("spread", g, j))
            spread(g, strip, j)
    for j in range(Z):
        for g in range(R):
            strip = strip_of(row_of(g), (z + Z - j) % Z, 1 - h)
            arrived(window_of(strip), ("spread_core", g, j))

    @pl.loop(0, blocks)
    def _(i):
        rows = pl.ds(pl.multiple_of(i * LANES, LANES), LANES)

        for d in range(1, half):
            to = pl.multiple_of(((i + d) % blocks) * LANES, LANES)
            block = cx[rows, pl.ds(pl.multiple_of((i + d) * LANES, LANES), LANES)]
            cx[pl.ds(to, LANES), rows] = block.T

    for i in range(half, blocks):
        rows = pl.ds(i * LANES, LANES)
        over = (i + half + 1 - blocks) * LANES
        cx[rows, :over] = cx[rows, n : n + over]

    for k in range(1, R):
        arrived(x0.at[:, columns_at((row + R - k) % R)], ("field", k))
    chunk = 4 * LANES
    for index in range(TERMS):
        source = x0 if index == 0 else xs.at[(index + 1) % 2]
        target = xs.at[index % 2]
        scale = 1.0 / (TERMS - index)

        @pl.loop(0, n // chunk)
        def _(c):
            columns = pl.ds(pl.multiple_of(c * chunk, chunk), chunk)
            product = jnp.dot(source[...], cx[:, columns], preferred_element_type=jnp.float32)
            target[:, columns] = (x0[:, columns].astype(jnp.float32) + scale * product).astype(jnp.bfloat16)

    last = xs.at[(TERMS - 1) % 2]
    for k in range(1, R):
        to = (row + k) % R
        send(last.at[:, columns_at(to)], ot.at[slab_at(row), :], (to, col), ("out", k))
    out_ref[slab_at(row), :] = last[:, columns_at(row)]
    for k in range(1, R):
        source = slab_at((row + R - k) % R)
        arrived(ot.at[source, :], ("out", k))
        out_ref[source, :] = ot[source, :]
    for copy in started:
        copy.wait_send()


def on_device(R, Z, mode_profiles, region_labels, gain_table, index_table, field_in):
    table = gain_table + index_table
    regions = jnp.arange(table.shape[0], dtype=jnp.int32)
    weight = jnp.sum(
        jnp.where(region_labels[:, None] == regions[None, :], table[None, :], 0.0), axis=1, keepdims=True
    )
    points, n = mode_profiles.shape
    width = n // 2 + LANES
    depth = n // (R * Z * 2)
    mine_cols = field_in.shape[1] // R
    messages = 2 * R * Z + 2 * (R - 1) * Z + 2 * (Z - 1) + 2 * (R - 1)
    bf16 = jnp.bfloat16
    turned = pl.pallas_call(
        functools.partial(kernel, R, Z, n),
        out_shape=jax.ShapeDtypeStruct(field_in.shape[::-1], bf16),
        in_specs=[pl.BlockSpec(memory_space=pltpu.VMEM)] * 3,
        out_specs=pl.BlockSpec(memory_space=pltpu.VMEM),
        scratch_shapes=[
            pltpu.VMEM((points, n + width - LANES), bf16),
            pltpu.VMEM((n, width), bf16),
            pltpu.VMEM((R * Z, depth, width), bf16),
            pltpu.VMEM(((R - 1) * Z, depth, width), bf16),
            pltpu.VMEM((Z - 1, depth, width), bf16),
            pltpu.VMEM((n, n + width - LANES), bf16),
            pltpu.VMEM((mine_cols, n), bf16),
            pltpu.VMEM((2, mine_cols, n), bf16),
            pltpu.VMEM(field_in.shape[::-1], bf16),
            pltpu.SemaphoreType.DMA((messages,)),
            pltpu.SemaphoreType.DMA((messages,)),
        ],
        compiler_params=pltpu.CompilerParams(
            collective_id=0, has_side_effects=True, vmem_limit_bytes=60 * 1024 * 1024),
    )(mode_profiles, weight, field_in.T)
    return turned.T


def solution(mesh):
    return jax.shard_map(
        functools.partial(on_device, mesh.shape["row"], mesh.shape["col"] // 2),
        mesh=mesh,
        in_specs=(P(("row", "col"), None), P(("row", "col")), P(), P(), P("row", "col")),
        out_specs=P("row", "col"),
        check_vma=False,
    )
```

```python
import functools

import jax
import jax.numpy as jnp
from jax import lax
from jax.experimental import pallas as pl
from jax.experimental.pallas import tpu as pltpu
from jax.sharding import PartitionSpec as P

TERMS = 6
LANES = 128
MESH = pl.DeviceIdType.MESH


def lowest_bit(g):
    t = 0
    while not (g >> t) & 1:
        t += 1
    return t


def kernel(R, Z, n, labels_ref, gain_ref, index_ref, p_hbm, f_ref, out_ref, p_ref, ft, s2, part, r0, rt, rz, cx, x0, xs, ot, send_sem, recv_sem, load_sem):
    bits = R.bit_length() - 1
    blocks = n // LANES
    half = blocks // 2
    width = (half + 1) * LANES
    depth = n // (R * Z * 2)
    mine_cols = x0.shape[0]
    row_rows = n // R
    row, col = lax.axis_index("row"), lax.axis_index("col")
    z, h = col // 2, col % 2
    partner = (row, z * 2 + 1 - h)

    def flip(r, t):
        mask0, mask1 = 1 << t, 1 << (bits - 1 - t)
        mask = mask0 + h * (mask1 - mask0)
        return r + mask * (1 - 2 * ((r // mask) % 2))

    def row_of(g):
        r = row
        for t in range(bits):
            if (g >> t) & 1:
                r = flip(r, t)
        return r

    def mirrored(g):
        return sum(((g >> t) & 1) << (bits - 1 - t) for t in range(bits))

    def z_of(j):
        return (z + 1 + j) % Z

    def strip_of(r, zz, hh):
        return (r * Z + zz) * 2 + hh

    def rows_of(ref, s):
        return ref.at[pl.ds(pl.multiple_of(s * depth, depth), depth), :]

    def window_of(s):
        start = pl.multiple_of((s * depth // LANES) * LANES, LANES)
        return cx.at[pl.ds(pl.multiple_of(s * depth, depth), depth), pl.ds(start, width)]

    ids, started = {}, []

    def slot(key):
        return ids.setdefault(key, len(ids))

    def send(src, dst, device, key):
        copy = pltpu.make_async_remote_copy(
            src_ref=src, dst_ref=dst, send_sem=send_sem.at[len(started)],
            recv_sem=recv_sem.at[slot(key)], device_id=device, device_id_type=MESH)
        copy.start()
        started.append(copy)

    def arrived(ref, key):
        pltpu.make_async_remote_copy(
            src_ref=ref, dst_ref=ref, send_sem=send_sem.at[0],
            recv_sem=recv_sem.at[slot(key)], device_id=partner, device_id_type=MESH).wait_recv()

    rows_at_once = LANES
    loads = p_ref.shape[0] // rows_at_once

    def load(i):
        rows = pl.ds(i * rows_at_once, rows_at_once)
        return pltpu.make_async_copy(p_hbm.at[rows, :], p_ref.at[rows, :], load_sem.at[i])

    for i in range(loads):
        load(i).start()

    barrier = pltpu.get_barrier_semaphore()
    peers = [((row + k) % R, col) for k in range(1, R)]
    peers += [(row, ((z + k) % Z) * 2 + h) for k in range(1, Z)] + [partner]
    for peer in peers:
        pl.semaphore_signal(barrier, inc=1, device_id=peer, device_id_type=MESH)
    pl.semaphore_wait(barrier, len(peers))

    def columns_at(r):
        return pl.ds(pl.multiple_of(r * row_rows, row_rows), row_rows)

    def slab_at(r):
        return pl.ds(pl.multiple_of(r * mine_cols, mine_cols), mine_cols)

    ft[...] = f_ref[...].T
    for k in range(1, R):
        to = (row + k) % R
        send(ft.at[slab_at(to), :], x0.at[:, columns_at(row)], (to, col), ("field", k))
    x0[:, columns_at(row)] = ft[slab_at(row), :]

    labels = labels_ref[...]
    weight = jnp.zeros(labels.shape, jnp.float32)
    for region in range(gain_ref.shape[0]):
        weight = jnp.where(labels == region, gain_ref[region] + index_ref[region], weight)
    for i in range(loads):
        rows = pl.ds(i * rows_at_once, rows_at_once)
        along = jnp.broadcast_to(weight[i : i + 1, :], (LANES, LANES)).T
        load(i).wait()
        for c in range(n // LANES):
            columns = pl.ds(c * LANES, LANES)
            scaled = (p_ref[rows, columns].astype(jnp.float32) * along).astype(jnp.bfloat16)
            s2[rows, columns] = scaled
            if c * LANES < width - LANES:
                s2[rows, pl.ds(n + c * LANES, LANES)] = scaled

    order = sorted(range(R), key=lambda g: (lowest_bit(g) if g else bits, -g))
    pair = 2 * LANES
    for g in order:
        r = row_of(g)

        @pl.loop(0, row_rows // pair)
        def _(q):
            base = pl.multiple_of(r * row_rows + q * pair, pair)
            left = p_ref[:, pl.ds(base, pair)].T
            both = jnp.dot(left, s2[:, pl.ds(base, width + LANES)], preferred_element_type=jnp.float32)
            part[pl.ds(base, LANES), :] = both[:LANES, :width].astype(jnp.bfloat16)
            part[pl.ds(base + LANES, LANES), :] = both[LANES:, LANES:].astype(jnp.bfloat16)

        for j in range(Z):
            send(rows_of(part, strip_of(r, z_of(j), 1 - h)), r0.at[mirrored(g) * Z + j], partner, ("core", mirrored(g), j))
            ids.setdefault(("core", g, j), len(ids))

    stage_slot = {}
    for t in range(bits):
        for g in range(R):
            if g % (2 << t) == 0:
                stage_slot[t, g] = len(stage_slot)

    for g in order:
        r = row_of(g)
        low = lowest_bit(g) if g else bits
        for j in range(Z):
            arrived(r0.at[g * Z + j], ("core", g, j))
            own = rows_of(part, strip_of(r, z_of(j), h))
            total = own[...].astype(jnp.float32) + r0[g * Z + j].astype(jnp.float32)
            for t in range(low):
                piece = rt.at[stage_slot[t, g] * Z + j]
                arrived(piece, ("row", t, g, j))
                total = total + piece[...].astype(jnp.float32)
            if g:
                own[...] = total.astype(jnp.bfloat16)
                seen = g ^ (1 << low)
                send(own, rt.at[stage_slot[low, seen] * Z + j], (flip(row, low), col), ("row", low, seen, j))
            elif j < Z - 1:
                own[...] = total.astype(jnp.bfloat16)
                send(own, rz.at[j], (row, z_of(j) * 2 + h), ("z", j))
            else:
                for i in range(Z - 1):
                    arrived(rz.at[i], ("z", i))
                    total = total + rz[i].astype(jnp.float32)
                window_of(strip_of(row, z, h))[...] = total.astype(jnp.bfloat16)

    def spread(g, strip, key_j):
        low = lowest_bit(g) if g else bits
        view = window_of(strip)
        for t in reversed(range(low)):
            send(view, view, (flip(row, t), col), ("spread", g | (1 << t), key_j))
        send(view, view, partner, ("spread_core", mirrored(g), key_j))

    def mirror_block(i):
        rows = pl.ds(pl.multiple_of(i * LANES, LANES), LANES)
        for d in range(1, half):
            to = pl.multiple_of(((i + d) % blocks) * LANES, LANES)
            block = cx[rows, pl.ds(pl.multiple_of((i + d) * LANES, LANES), LANES)]
            cx[pl.ds(to, LANES), rows] = block.T

    def source_z(j):
        return (z + Z - j) % Z

    mine = window_of(strip_of(row, z, h))
    for j in range(Z - 1):
        send(mine, mine, (row, z_of(j) * 2 + h), ("spread", 0, j + 1))

    def tick(at):
        g, j = at
        low = lowest_bit(g) if g else bits
        return j + bin(g).count("1") + (low == 0), -low

    per_chip = 2 * depth == LANES
    schedule = sorted(((g, j) for g in range(R) for j in range(Z)), key=tick)
    lag = 3
    here, there = set(), set()
    for step in range(len(schedule) + lag):
        touched = []
        if step < len(schedule):
            g, j = schedule[step]
            strip = strip_of(row_of(g), source_z(j), h)
            if g or j:
                arrived(window_of(strip), ("spread", g, j))
            spread(g, strip, j)
            here.add((g, j))
            touched.append((g, j))
        if step >= lag:
            g, j = schedule[step - lag]
            g = mirrored(g)
            arrived(window_of(strip_of(row_of(g), source_z(j), 1 - h)), ("spread_core", g, j))
            there.add((g, j))
            touched.append((g, j))
        for g, j in touched:
            if per_chip and (g, j) in here and (g, j) in there:
                mirror_block(row_of(g) * Z + source_z(j))
    if not per_chip:
        pl.loop(0, blocks)(mirror_block)

    for i in range(half, blocks):
        rows = pl.ds(i * LANES, LANES)
        over = (i + half + 1 - blocks) * LANES
        cx[rows, :over] = cx[rows, n : n + over]

    for k in range(1, R):
        arrived(x0.at[:, columns_at((row + R - k) % R)], ("field", k))
    chunk = 4 * LANES
    for index in range(TERMS):
        source = x0 if index == 0 else xs.at[(index + 1) % 2]
        target = xs.at[index % 2]
        scale = 1.0 / (TERMS - index)

        @pl.loop(0, n // chunk)
        def _(c):
            columns = pl.ds(pl.multiple_of(c * chunk, chunk), chunk)
            product = jnp.dot(source[...], cx[:, columns], preferred_element_type=jnp.float32)
            target[:, columns] = (x0[:, columns].astype(jnp.float32) + scale * product).astype(jnp.bfloat16)

    last = xs.at[(TERMS - 1) % 2]
    for k in range(1, R):
        to = (row + k) % R
        send(last.at[:, columns_at(to)], ot.at[slab_at(row), :], (to, col), ("out", k))
    out_ref[slab_at(row), :] = last[:, columns_at(row)]
    for k in range(1, R):
        source = slab_at((row + R - k) % R)
        arrived(ot.at[source, :], ("out", k))
        out_ref[source, :] = ot[source, :]
    for copy in started:
        copy.wait_send()


def on_device(R, Z, mode_profiles, region_labels, gain_table, index_table, field_in):
    points, n = mode_profiles.shape
    width = n // 2 + LANES
    depth = n // (R * Z * 2)
    mine_cols = field_in.shape[1] // R
    messages = 2 * R * Z + 2 * (R - 1) * Z + 2 * (Z - 1) + 2 * (R - 1)
    bf16 = jnp.bfloat16
    turned = pl.pallas_call(
        functools.partial(kernel, R, Z, n),
        out_shape=jax.ShapeDtypeStruct(field_in.shape[::-1], bf16),
        in_specs=[
            pl.BlockSpec(memory_space=pltpu.VMEM),
            pl.BlockSpec(memory_space=pltpu.SMEM),
            pl.BlockSpec(memory_space=pltpu.SMEM),
            pl.BlockSpec(memory_space=pl.ANY),
            pl.BlockSpec(memory_space=pltpu.VMEM),
        ],
        out_specs=pl.BlockSpec(memory_space=pltpu.VMEM),
        scratch_shapes=[
            pltpu.VMEM((points, n), bf16),
            pltpu.VMEM(field_in.shape[::-1], bf16),
            pltpu.VMEM((points, n + width - LANES), bf16),
            pltpu.VMEM((n, width), bf16),
            pltpu.VMEM((R * Z, depth, width), bf16),
            pltpu.VMEM(((R - 1) * Z, depth, width), bf16),
            pltpu.VMEM((Z - 1, depth, width), bf16),
            pltpu.VMEM((n, n + width - LANES), bf16),
            pltpu.VMEM((mine_cols, n), bf16),
            pltpu.VMEM((2, mine_cols, n), bf16),
            pltpu.VMEM(field_in.shape[::-1], bf16),
            pltpu.SemaphoreType.DMA((messages,)),
            pltpu.SemaphoreType.DMA((messages,)),
            pltpu.SemaphoreType.DMA((points // LANES,)),
        ],
        compiler_params=pltpu.CompilerParams(
            collective_id=0, has_side_effects=True, vmem_limit_bytes=60 * 1024 * 1024),
    )(region_labels.reshape(-1, LANES), gain_table, index_table, mode_profiles, field_in)
    return turned.T


def solution(mesh):
    return jax.shard_map(
        functools.partial(on_device, mesh.shape["row"], mesh.shape["col"] // 2),
        mesh=mesh,
        in_specs=(P(("row", "col"), None), P(("row", "col")), P(), P(), P("row", "col")),
        out_specs=P("row", "col"),
        check_vma=False,
    )
```

```python
import functools

import jax
import jax.numpy as jnp
from jax import lax
from jax.experimental import pallas as pl
from jax.experimental.pallas import tpu as pltpu
from jax.sharding import PartitionSpec as P

TERMS = 6
LANES = 128
MESH = pl.DeviceIdType.MESH


def lowest_bit(g):
    t = 0
    while not (g >> t) & 1:
        t += 1
    return t


def kernel(R, Z, n, labels_ref, gain_ref, index_ref, p_hbm, f_ref, out_ref, p_ref, ft, s2, part, r0, rt, rz, cx, x0, xs, ot, send_sem, recv_sem, load_sem):
    bits = R.bit_length() - 1
    blocks = n // LANES
    half = blocks // 2
    width = (half + 1) * LANES
    depth = n // (R * Z * 2)
    mine_cols = x0.shape[0]
    row_rows = n // R
    row, col = lax.axis_index("row"), lax.axis_index("col")
    z, h = col // 2, col % 2
    partner = (row, z * 2 + 1 - h)

    def flip(r, t):
        mask0, mask1 = 1 << t, 1 << (bits - 1 - t)
        mask = mask0 + h * (mask1 - mask0)
        return r + mask * (1 - 2 * ((r // mask) % 2))

    def row_of(g):
        r = row
        for t in range(bits):
            if (g >> t) & 1:
                r = flip(r, t)
        return r

    def mirrored(g):
        return sum(((g >> t) & 1) << (bits - 1 - t) for t in range(bits))

    def z_of(j):
        return (z + 1 + j) % Z

    def strip_of(r, zz, hh):
        return (r * Z + zz) * 2 + hh

    def rows_of(ref, s):
        return ref.at[pl.ds(pl.multiple_of(s * depth, depth), depth), :]

    def window_of(s):
        start = pl.multiple_of((s * depth // LANES) * LANES, LANES)
        return cx.at[pl.ds(pl.multiple_of(s * depth, depth), depth), pl.ds(start, width)]

    ids, started = {}, []

    def slot(key):
        return ids.setdefault(key, len(ids))

    def send(src, dst, device, key):
        copy = pltpu.make_async_remote_copy(
            src_ref=src, dst_ref=dst, send_sem=send_sem.at[len(started)],
            recv_sem=recv_sem.at[slot(key)], device_id=device, device_id_type=MESH)
        copy.start()
        started.append(copy)

    def arrived(ref, key):
        pltpu.make_async_remote_copy(
            src_ref=ref, dst_ref=ref, send_sem=send_sem.at[0],
            recv_sem=recv_sem.at[slot(key)], device_id=partner, device_id_type=MESH).wait_recv()

    rows_at_once = LANES
    loads = p_ref.shape[0] // rows_at_once

    def load(i):
        rows = pl.ds(i * rows_at_once, rows_at_once)
        return pltpu.make_async_copy(p_hbm.at[rows, :], p_ref.at[rows, :], load_sem.at[i])

    for i in range(loads):
        load(i).start()

    barrier = pltpu.get_barrier_semaphore()
    peers = [((row + k) % R, col) for k in range(1, R)]
    peers += [(row, ((z + k) % Z) * 2 + h) for k in range(1, Z)] + [partner]
    for peer in peers:
        pl.semaphore_signal(barrier, inc=1, device_id=peer, device_id_type=MESH)

    def columns_at(r):
        return pl.ds(pl.multiple_of(r * row_rows, row_rows), row_rows)

    def slab_at(r):
        return pl.ds(pl.multiple_of(r * mine_cols, mine_cols), mine_cols)

    ft[...] = f_ref[...].T
    labels = labels_ref[...]
    weight = jnp.zeros(labels.shape, jnp.float32)
    for region in range(gain_ref.shape[0]):
        weight = jnp.where(labels == region, gain_ref[region] + index_ref[region], weight)
    for i in range(loads):
        rows = pl.ds(i * rows_at_once, rows_at_once)
        along = jnp.broadcast_to(weight[i : i + 1, :], (LANES, LANES)).T
        load(i).wait()
        for c in range(n // LANES):
            columns = pl.ds(c * LANES, LANES)
            scaled = (p_ref[rows, columns].astype(jnp.float32) * along).astype(jnp.bfloat16)
            s2[rows, columns] = scaled
            if c * LANES < width - LANES:
                s2[rows, pl.ds(n + c * LANES, LANES)] = scaled

    order = sorted(range(R), key=lambda g: (lowest_bit(g) if g else bits, -g))
    stage_slot = {}
    for t in range(bits):
        for g in range(R):
            if g % (2 << t) == 0:
                stage_slot[t, g] = len(stage_slot)

    def reduce_group(g):
        r = row_of(g)
        low = lowest_bit(g) if g else bits
        for j in range(Z):
            arrived(r0.at[g * Z + j], ("core", g, j))
            own = rows_of(part, strip_of(r, z_of(j), h))
            total = own[...].astype(jnp.float32) + r0[g * Z + j].astype(jnp.float32)
            for t in range(low):
                piece = rt.at[stage_slot[t, g] * Z + j]
                arrived(piece, ("row", t, g, j))
                total = total + piece[...].astype(jnp.float32)
            if g:
                own[...] = total.astype(jnp.bfloat16)
                seen = g ^ (1 << low)
                send(own, rt.at[stage_slot[low, seen] * Z + j], (flip(row, low), col), ("row", low, seen, j))
            elif j < Z - 1:
                own[...] = total.astype(jnp.bfloat16)
                send(own, rz.at[j], (row, z_of(j) * 2 + h), ("z", j))
            else:
                for i in range(Z - 1):
                    arrived(rz.at[i], ("z", i))
                    total = total + rz[i].astype(jnp.float32)
                window_of(strip_of(row, z, h))[...] = total.astype(jnp.bfloat16)

    pair = 2 * LANES
    waiting = list(order)
    for at, g in enumerate(order):
        r = row_of(g)

        @pl.loop(0, row_rows // pair)
        def _(q):
            base = pl.multiple_of(r * row_rows + q * pair, pair)
            left = p_ref[:, pl.ds(base, pair)].T
            both = jnp.dot(left, s2[:, pl.ds(base, width + LANES)], preferred_element_type=jnp.float32)
            part[pl.ds(base, LANES), :] = both[:LANES, :width].astype(jnp.bfloat16)
            part[pl.ds(base + LANES, LANES), :] = both[LANES:, LANES:].astype(jnp.bfloat16)

        if at == 0:
            pl.semaphore_wait(barrier, len(peers))
        for j in range(Z):
            send(rows_of(part, strip_of(r, z_of(j), 1 - h)), r0.at[mirrored(g) * Z + j], partner, ("core", mirrored(g), j))
        while waiting and order.index(waiting[0]) < at and order.index(mirrored(waiting[0])) <= at:
            reduce_group(waiting.pop(0))
    for g in waiting:
        reduce_group(g)

    for k in range(1, R):
        to = (row + k) % R
        send(ft.at[slab_at(to), :], x0.at[:, columns_at(row)], (to, col), ("field", k))
    x0[:, columns_at(row)] = ft[slab_at(row), :]

    def spread(g, strip, key_j):
        low = lowest_bit(g) if g else bits
        view = window_of(strip)
        for t in reversed(range(low)):
            send(view, view, (flip(row, t), col), ("spread", g | (1 << t), key_j))
        send(view, view, partner, ("spread_core", mirrored(g), key_j))

    def mirror_block(i):
        rows = pl.ds(pl.multiple_of(i * LANES, LANES), LANES)
        for d in range(1, half):
            to = pl.multiple_of(((i + d) % blocks) * LANES, LANES)
            block = cx[rows, pl.ds(pl.multiple_of((i + d) * LANES, LANES), LANES)]
            cx[pl.ds(to, LANES), rows] = block.T

    def source_z(j):
        return (z + Z - j) % Z

    mine = window_of(strip_of(row, z, h))
    for j in range(Z - 1):
        send(mine, mine, (row, z_of(j) * 2 + h), ("spread", 0, j + 1))

    def tick(at):
        g, j = at
        low = lowest_bit(g) if g else bits
        return j + bin(g).count("1") + (low == 0), -low

    per_chip = 2 * depth == LANES
    schedule = sorted(((g, j) for g in range(R) for j in range(Z)), key=tick)
    lag = 3
    here, there = set(), set()
    for step in range(len(schedule) + lag):
        touched = []
        if step < len(schedule):
            g, j = schedule[step]
            strip = strip_of(row_of(g), source_z(j), h)
            if g or j:
                arrived(window_of(strip), ("spread", g, j))
            spread(g, strip, j)
            here.add((g, j))
            touched.append((g, j))
        if step >= lag:
            g, j = schedule[step - lag]
            g = mirrored(g)
            arrived(window_of(strip_of(row_of(g), source_z(j), 1 - h)), ("spread_core", g, j))
            there.add((g, j))
            touched.append((g, j))
        for g, j in touched:
            if per_chip and (g, j) in here and (g, j) in there:
                mirror_block(row_of(g) * Z + source_z(j))
    if not per_chip:
        pl.loop(0, blocks)(mirror_block)

    for i in range(half, blocks):
        rows = pl.ds(i * LANES, LANES)
        over = (i + half + 1 - blocks) * LANES
        cx[rows, :over] = cx[rows, n : n + over]

    for k in range(1, R):
        arrived(x0.at[:, columns_at((row + R - k) % R)], ("field", k))
    for index in range(TERMS):
        source = x0 if index == 0 else xs.at[(index + 1) % 2]
        target = xs.at[index % 2]
        scale = 1.0 / (TERMS - index)

        product = jnp.dot(source[...], cx[:, :n], preferred_element_type=jnp.float32)
        target[...] = (x0[...].astype(jnp.float32) + scale * product).astype(jnp.bfloat16)

    last = xs.at[(TERMS - 1) % 2]
    for k in range(1, R):
        to = (row + k) % R
        send(last.at[:, columns_at(to)], ot.at[slab_at(row), :], (to, col), ("out", k))
    out_ref[slab_at(row), :] = last[:, columns_at(row)]
    for k in range(1, R):
        source = slab_at((row + R - k) % R)
        arrived(ot.at[source, :], ("out", k))
        out_ref[source, :] = ot[source, :]
    for copy in started:
        copy.wait_send()


def on_device(R, Z, mode_profiles, region_labels, gain_table, index_table, field_in):
    points, n = mode_profiles.shape
    width = n // 2 + LANES
    depth = n // (R * Z * 2)
    mine_cols = field_in.shape[1] // R
    messages = 2 * R * Z + 2 * (R - 1) * Z + 2 * (Z - 1) + 2 * (R - 1)
    bf16 = jnp.bfloat16
    turned = pl.pallas_call(
        functools.partial(kernel, R, Z, n),
        out_shape=jax.ShapeDtypeStruct(field_in.shape[::-1], bf16),
        in_specs=[
            pl.BlockSpec(memory_space=pltpu.VMEM),
            pl.BlockSpec(memory_space=pltpu.SMEM),
            pl.BlockSpec(memory_space=pltpu.SMEM),
            pl.BlockSpec(memory_space=pl.ANY),
            pl.BlockSpec(memory_space=pltpu.VMEM),
        ],
        out_specs=pl.BlockSpec(memory_space=pltpu.VMEM),
        scratch_shapes=[
            pltpu.VMEM((points, n), bf16),
            pltpu.VMEM(field_in.shape[::-1], bf16),
            pltpu.VMEM((points, n + width - LANES), bf16),
            pltpu.VMEM((n, width), bf16),
            pltpu.VMEM((R * Z, depth, width), bf16),
            pltpu.VMEM(((R - 1) * Z, depth, width), bf16),
            pltpu.VMEM((Z - 1, depth, width), bf16),
            pltpu.VMEM((n, n + width - LANES), bf16),
            pltpu.VMEM((mine_cols, n), bf16),
            pltpu.VMEM((2, mine_cols, n), bf16),
            pltpu.VMEM(field_in.shape[::-1], bf16),
            pltpu.SemaphoreType.DMA((messages,)),
            pltpu.SemaphoreType.DMA((messages,)),
            pltpu.SemaphoreType.DMA((points // LANES,)),
        ],
        compiler_params=pltpu.CompilerParams(
            collective_id=0, has_side_effects=True, vmem_limit_bytes=60 * 1024 * 1024),
    )(region_labels.reshape(-1, LANES), gain_table, index_table, mode_profiles, field_in)
    return turned.T


def solution(mesh):
    return jax.shard_map(
        functools.partial(on_device, mesh.shape["row"], mesh.shape["col"] // 2),
        mesh=mesh,
        in_specs=(P(("row", "col"), None), P(("row", "col")), P(), P(), P("row", "col")),
        out_specs=P("row", "col"),
        check_vma=False,
    )
```
